256 devices in a mesh: dp: 4 (over x), expert: 64 (over z, y, core).
Axes of the slice: x: 4, y: 4, z: 8, core: 2. Of those that a mesh axis runs over, the one named last changes fastest.
Arguments:
- tokens: bfloat16 [4096, 3584], P('expert'), may hold values from -6 to 6
- expert_ids: int32 [4096, 8], P('expert'), may hold values from 0 to 63, all different within a row; in each aligned block of 64 rows (0 to 63, 64 to 127, ...) at most 8 rows name the same one
- weight_num: int32 [4096, 8], P('expert'), may hold values from 64 to 1023
- gate_proj: bfloat16 [64, 3584, 2048], P('expert', None, 'dp'), may hold values from -0.09375 to 0.09375
- up_proj: bfloat16 [64, 3584, 2048], P('expert', None, 'dp'), may hold values from -0.09375 to 0.09375
- down_proj: bfloat16 [64, 2048, 3584], P('expert', 'dp'), may hold values from -0.125 to 0.125
Outputs:
- combined: bfloat16 [4096, 3584], P('expert', 'dp')
The draws below stay inside these ranges and needn't reach their ends.
Inputs may be any that keep to these rules, and one draw needn't show every extreme that they name: `expert_ids`: in the 64 rows of one device no expert is named by more than 8 rows, and some device has an expert named by exactly 8 of its rows.
All inputs are finite; a program needn't handle non-finite values.
Results may differ from the reference program's by a relative error of at most 0.015.
Values may be sent and summed in bfloat16 or wider, within the bound.
A program may use at most 192 MiB of HBM per device.

```python
import math
import jax
import jax.numpy as jnp
import numpy as np
from jax import lax

D = 3584
F = 2048
TOP = 8
TOK_DEV = 64
EXPERTS = 64
TOKENS = 4096
SHARE = 512
CAP = 8
N_DP = 4
N_EXPERT = 64


def plant(drawn, own_key, smallest, largest):
    shape = drawn.shape
    place = [jax.random.randint(jax.random.fold_in(own_key, axis), (), 0, shape[axis]) for axis in range(len(shape))]
    drawn = drawn.at[tuple(place)].set(smallest)
    longest = shape.index(max(shape))
    place[longest] = (place[longest] + 1) % shape[longest]
    return drawn.at[tuple(place)].set(largest)


def levels(rng, shape, shards, low, high):
    factor_of = 1.0
    for dim, parts in shards:
        draws = jax.random.uniform(jax.random.fold_in(jax.random.fold_in(rng, 6), dim), (parts,), jnp.float32, low / len(shards), high / len(shards))
        factor_of = factor_of * jnp.repeat(jnp.exp(draws), shape[dim] // parts).reshape((-1,) + (1,) * (len(shape) - 1 - dim))
    return factor_of


def deal_out(stream_key, own, number, rows, amount, top, reach, lean):
    order = jax.random.permutation(stream_key, amount)
    packed, usual = load_shares(amount, rows * top, reach, lean, True), load_shares(amount, rows * top, reach, lean, False)
    places = jnp.arange(amount)

    def named(sizes, rotation):
        used = int((sizes > 0).sum())
        fixed = max(1, used // 4)
        passed = fixed + (places - fixed + rotation * (used - fixed)) % max(1, amount - fixed)
        return jnp.zeros((amount,), jnp.int32).at[order[jnp.where(places < fixed, places, passed)]].set(jnp.asarray(sizes, jnp.int32))

    sizes = jnp.where(number % 4 == 0, named(packed, number // 4), named(usual, number - number // 4 - 1))
    mixed = jax.random.permutation(jax.random.fold_in(own, 3), amount)
    source_of, sink = mixed[0:amount // 2 * 2:2], mixed[1:amount // 2 * 2:2]
    margin = jnp.minimum(sizes[source_of] - 1, reach - sizes[sink]) // 2
    margin = jnp.where((source_of == order[0]) | (sink == order[0]) | (sizes[sink] == 0), 0, jnp.maximum(margin, 0))
    passed = jax.random.randint(jax.random.fold_in(own, 4), (amount // 2,), 0, 1 << 20) % (margin + 1)
    sizes = sizes.at[source_of].add(-passed).at[sink].add(passed)
    members = jnp.searchsorted(jnp.cumsum(sizes), jnp.arange(rows * top), side="right").astype(jnp.int32)
    table = members.reshape(top, rows).T
    table = table[jax.random.permutation(jax.random.fold_in(own, 1), rows)]
    rotation = jax.random.randint(jax.random.fold_in(own, 2), (rows, 1), 0, top)
    return jnp.take_along_axis(table, (jnp.arange(top)[None, :] + rotation) % top, axis=1)


def load_shares(number_of, total, reach, slope, full):
    loads = [(1 << 20) // math.isqrt(grade ** slope) + 1 for grade in range(1, number_of + 1)]
    largest = reach if full else min(reach, max(-(-total // number_of), total * loads[0] // sum(loads)))
    least = 1 if total - largest >= number_of - 1 else 0
    holding, rest = [largest] + [least] * (number_of - 1), total - largest - least * (number_of - 1)
    while rest > 0:
        candidates = [i for i in range(1, number_of) if holding[i] < largest] or [i for i in range(1, number_of) if holding[i] < reach]
        mass, remaining = sum([loads[i] for i in candidates]), rest
        for i in candidates:
            more = min(reach - holding[i], max(1, remaining * loads[i] // mass), rest)
            holding[i] = holding[i] + more
            rest = rest - more
    return np.array(holding)


def centred(own_key, extent, scale, most, cuts=(), kind=jnp.bfloat16):
    array = scale * jax.random.normal(own_key, extent, jnp.float32)
    if cuts:
        array = array * levels(own_key, extent, cuts, -0.22, 0.18)
    return jnp.clip(array, -most, most).astype(kind)


def setup_inputs(seed: int = 0) -> dict:
    arg_keys = jax.random.split(jax.random.key(seed), 7)
    tokens = centred(arg_keys[0], (TOKENS, D), 1.0, 6.0, ((0, 64),))
    expert_ids_keys = jax.random.split(jax.random.fold_in(arg_keys[1], 1), TOKENS // TOK_DEV)
    expert_ids_turns = jax.random.permutation(jax.random.fold_in(arg_keys[1], 3), TOKENS // TOK_DEV)
    expert_ids = jax.vmap(lambda own, number: deal_out(jax.random.fold_in(arg_keys[1], 2), own, number, TOK_DEV, EXPERTS, TOP, CAP, 1))(expert_ids_keys, expert_ids_turns).reshape((TOKENS, TOP))
    weight_num = plant(jax.random.randint(arg_keys[2], (TOKENS, TOP), 64, 1024), jax.random.fold_in(arg_keys[2], 1), 64, 1023).astype(jnp.int32)
    gate_proj = centred(arg_keys[3], (EXPERTS, D, F), D ** -0.5, 0.09375, ((0, 64), (2, 4)))
    up_proj = centred(arg_keys[4], (EXPERTS, D, F), D ** -0.5, 0.09375, ((0, 64), (2, 4)))
    down_proj = centred(arg_keys[5], (EXPERTS, F, D), F ** -0.5, 0.125, ((0, 64), (1, 4)))
    return dict(tokens=tokens, expert_ids=expert_ids, weight_num=weight_num, gate_proj=gate_proj, up_proj=up_proj, down_proj=down_proj)


def routing_table(block_ids, expert_total, capacity):
    row_count = block_ids.shape[0]
    top_count = block_ids.shape[1]
    flat_ids = block_ids.reshape(-1)
    onehot = (flat_ids[:, None] == jnp.arange(expert_total, dtype=jnp.int32)[None, :]).astype(jnp.int32)
    before = jnp.cumsum(onehot, axis=0) - onehot
    position = jnp.sum(before * onehot, axis=1).astype(jnp.int32)
    target = (flat_ids * capacity + position).astype(jnp.int32)
    owners = jnp.full((expert_total * capacity,), row_count * top_count, jnp.int32)
    owners = owners.at[target].set(jnp.arange(row_count * top_count, dtype=jnp.int32))
    return target, owners


def reference(tokens, expert_ids, weight_num, gate_proj, up_proj, down_proj):
    blocks = N_EXPERT
    pairs = TOK_DEV * TOP
    owners = jax.vmap(lambda block_ids: routing_table(block_ids, EXPERTS, CAP)[1])(expert_ids.reshape(blocks, TOK_DEV, TOP))
    weights = weight_num.astype(jnp.float32) / 1024.0
    flat_weight = weights.reshape(blocks, pairs)
    block_start = (jnp.arange(blocks, dtype=jnp.int32) * TOK_DEV).astype(jnp.int32)

    def per_expert(accum_out, expert_index):
        slot_owner = lax.dynamic_slice_in_dim(owners, (expert_index * CAP).astype(jnp.int32), CAP, 1)
        usable = slot_owner < pairs
        safe_slot = jnp.where(usable, slot_owner, 0).astype(jnp.int32)
        token_rows = (block_start[:, None] + safe_slot // TOP).reshape(-1).astype(jnp.int32)
        slot_weight = (jnp.take_along_axis(flat_weight, safe_slot, axis=1) * usable.astype(jnp.float32)).reshape(-1)
        picked = tokens[token_rows]
        gate_out = jnp.dot(picked, gate_proj[expert_index], preferred_element_type=jnp.float32)
        up_out = jnp.dot(picked, up_proj[expert_index], preferred_element_type=jnp.float32)
        hidden = (jax.nn.silu(gate_out) * up_out).astype(jnp.bfloat16)
        down_rows = down_proj[expert_index]
        expert_out = jnp.zeros((token_rows.shape[0], D), jnp.float32)
        for share_index in range(N_DP):
            share_out = jnp.dot(hidden[:, share_index * SHARE:(share_index + 1) * SHARE], down_rows[share_index * SHARE:(share_index + 1) * SHARE, :], preferred_element_type=jnp.float32).astype(jnp.bfloat16)
            share_out = lax.optimization_barrier(share_out)
            expert_out = expert_out + share_out.astype(jnp.float32)
        accum_out = accum_out.at[token_rows].add(slot_weight[:, None] * expert_out)
        return accum_out, None

    accum_out, _ = lax.scan(per_expert, jnp.zeros((TOKENS, D), jnp.float32), jnp.arange(EXPERTS, dtype=jnp.int32))
    return accum_out.astype(jnp.bfloat16)
```

```python
import jax
import jax.numpy as jnp
from jax import lax
from jax.sharding import PartitionSpec as P

ROOM = 8


def slot_matrices(ids, num, experts, capacity):
    rows = ids.shape[0]
    slots = experts * capacity
    column = jnp.arange(slots, dtype=jnp.int32)[None, :]
    expert_of = column // capacity
    hits = [ids[:, k : k + 1] == expert_of for k in range(ids.shape[1])]
    named = sum(h.astype(jnp.float32) for h in hits)
    weight = sum(jnp.where(h, num[:, k : k + 1], 0) for k, h in enumerate(hits))
    earlier = jnp.arange(rows)[:, None] > jnp.arange(rows)[None, :]
    position = jnp.dot(
        earlier.astype(jnp.bfloat16), named.astype(jnp.bfloat16), preferred_element_type=jnp.float32
    )
    here = (named > 0) & (position == (column % capacity).astype(jnp.float32))
    high = jnp.where(here, weight // 32 * 32, 0).astype(jnp.bfloat16)
    low = jnp.where(here, weight % 32, 0).astype(jnp.bfloat16)
    return here.astype(jnp.bfloat16), high, low


def local(tokens, expert_ids, weight_num, gate_proj, up_proj, down_proj):
    experts = lax.axis_size("expert")
    parts = lax.axis_size("dp")
    width = tokens.shape[1]
    quarter = width // parts
    slots = experts * ROOM
    here, high, low = slot_matrices(expert_ids, weight_num, experts, ROOM)
    mine = lax.dynamic_slice_in_dim(tokens, lax.axis_index("dp") * quarter, quarter, 1)
    outgoing = lax.dot_general(
        here, mine, (((0,), (0,)), ((), ())), preferred_element_type=jnp.float32
    ).astype(jnp.bfloat16)
    arrived = lax.all_to_all(
        outgoing.reshape(experts, ROOM, quarter), "expert", split_axis=0, concat_axis=0, tiled=True
    ).reshape(slots, quarter)
    rows = lax.all_gather(arrived, "dp", axis=0, tiled=True)
    gate_out, up_out = 0.0, 0.0
    for q in range(parts):
        block = rows[q * slots : (q + 1) * slots]
        cut = slice(q * quarter, (q + 1) * quarter)
        gate_out += jnp.dot(block, gate_proj[0, cut], preferred_element_type=jnp.float32)
        up_out += jnp.dot(block, up_proj[0, cut], preferred_element_type=jnp.float32)
    hidden = (jax.nn.silu(gate_out) * up_out).astype(jnp.bfloat16)
    partial = jnp.concatenate(
        [
            jnp.dot(
                hidden,
                down_proj[0, :, q * quarter : (q + 1) * quarter],
                preferred_element_type=jnp.float32,
            ).astype(jnp.bfloat16)
            for q in range(parts)
        ],
        axis=0,
    )
    summed = lax.psum_scatter(partial, "dp", scatter_dimension=0, tiled=True)
    returned = lax.all_to_all(
        summed.reshape(experts, ROOM, quarter), "expert", split_axis=0, concat_axis=0, tiled=True
    ).reshape(slots, quarter)
    total = jnp.dot(high, returned, preferred_element_type=jnp.float32)
    total += jnp.dot(low, returned, preferred_element_type=jnp.float32)
    return (total / 1024.0).astype(jnp.bfloat16)


def solution(mesh):
    placed = (
        P("expert", None),
        P("expert", None),
        P("expert", None),
        P("expert", None, "dp"),
        P("expert", None, "dp"),
        P("expert", "dp", None),
    )
    return jax.shard_map(
        local, mesh=mesh, in_specs=placed, out_specs=P("expert", "dp"), check_vma=False
    )
```
